32 devices in a mesh: expert: 4 (over z), tensor: 4 (over y, x), dp: 2 (over core).
Axes of the slice: x: 2, y: 2, z: 4, core: 2. Of those that a mesh axis runs over, the one named last changes fastest.
Arguments:
- tokens: bfloat16 [4096, 2048], P(('dp', 'expert', 'tensor')), parts along dimension 0, may hold values from -6 to 6
- expert_ids: int32 [4096, 4], P(('dp', 'expert', 'tensor')), parts along dimension 0, may hold values from 0 to 15, all different within a row; in each aligned block of 128 rows (0 to 127, 128 to 255, ...) at most 64 rows name the same one
- gate_probs: float32 [4096, 4], P(('dp', 'expert', 'tensor')), parts along dimension 0, may hold values from 0.05 to 0.6
- w_gate: bfloat16 [16, 2048, 1408], P(('expert', 'tensor')), may hold values from -0.125 to 0.125
- w_up: bfloat16 [16, 2048, 1408], P(('expert', 'tensor')), may hold values from -0.125 to 0.125
- w_down: bfloat16 [16, 1408, 2048], P(('expert', 'tensor')), may hold values from -0.15625 to 0.15625
- s_gate: bfloat16 [2048, 2816], P(None, 'tensor'), may hold values from -0.125 to 0.125
- s_up: bfloat16 [2048, 2816], P(None, 'tensor'), may hold values from -0.125 to 0.125
- s_down: bfloat16 [2816, 2048], P('tensor'), may hold values from -0.109375 to 0.109375
- shared_gate: bfloat16 [2048], replicated, may hold values from -0.125 to 0.125
Outputs:
- mixed: bfloat16 [4096, 2048], P(('dp', 'expert', 'tensor')), parts along dimension 0
The draws below stay inside these ranges and needn't reach their ends.
There are 2 independent parts, one for each index of `dp`. The reference program is written for one: setup_inputs(seed, part) draws one part's arguments, and reference() takes and returns one part's arrays. A program takes and returns all parts, laid end to end along the dimension named above; an argument that names none is the same for every part. Nothing has to cross between parts.
Inputs may be any that keep to these rules, and one draw needn't show every extreme that they name: `expert_ids`: among the rows of one device, no expert is named by more than 64 of them.
All inputs are finite; a program needn't handle non-finite values.
Results may differ from the reference program's by a relative error of at most 0.0095.
Values may be sent and summed in bfloat16 or wider, within the bound.
A program may use at most 128 MiB of HBM per device.

```python
import math
import jax
import jax.numpy as jnp
import numpy as np
from jax import lax

D = 2048
F = 1408
FS = 2816
TOP = 4
TOK_DEV = 128
EXPERTS = 16
CAP = 64
TOKENS = 2048
N_EXPERT = 4
N_TENSOR = 4


def level_of(rng, extent, shards, least, largest):
    factor_of = 1.0
    for position, blocks in shards:
        draws = jax.random.uniform(jax.random.fold_in(jax.random.fold_in(rng, 6), position), (blocks,), jnp.float32, least / len(shards), largest / len(shards))
        factor_of = factor_of * jnp.repeat(jnp.exp(draws), extent[position] // blocks).reshape((-1,) + (1,) * (len(extent) - 1 - position))
    return factor_of


def assign_block(own_key, own, number, rows, amount, top, bound, slope):
    sequence = jax.random.permutation(own_key, amount)
    crowded, common = load_shares(amount, rows * top, bound, slope, True), load_shares(amount, rows * top, bound, slope, False)
    places = jnp.arange(amount)

    def named(lengths, rotation):
        used = int((lengths > 0).sum())
        fixed = max(1, used // 4)
        shifted = fixed + (places - fixed + rotation * (used - fixed)) % max(1, amount - fixed)
        return jnp.zeros((amount,), jnp.int32).at[sequence[jnp.where(places < fixed, places, shifted)]].set(jnp.asarray(lengths, jnp.int32))

    lengths = jnp.where(number % 4 == 0, named(crowded, number // 4), named(common, number - number // 4 - 1))
    mixed = jax.random.permutation(jax.random.fold_in(own, 3), amount)
    donor, taker = mixed[0:amount // 2 * 2:2], mixed[1:amount // 2 * 2:2]
    room = jnp.minimum(lengths[donor] - 1, bound - lengths[taker]) // 2
    room = jnp.where((donor == sequence[0]) | (taker == sequence[0]) | (lengths[taker] == 0), 0, jnp.maximum(room, 0))
    shifted = jax.random.randint(jax.random.fold_in(own, 4), (amount // 2,), 0, 1 << 20) % (room + 1)
    lengths = lengths.at[donor].add(-shifted).at[taker].add(shifted)
    items = jnp.searchsorted(jnp.cumsum(lengths), jnp.arange(rows * top), side="right").astype(jnp.int32)
    grid = items.reshape(top, rows).T
    grid = grid[jax.random.permutation(jax.random.fold_in(own, 1), rows)]
    rotation = jax.random.randint(jax.random.fold_in(own, 2), (rows, 1), 0, top)
    return jnp.take_along_axis(grid, (jnp.arange(top)[None, :] + rotation) % top, axis=1)


def load_shares(number_of, total, most, skew, full):
    weights = [(1 << 20) // math.isqrt(grade ** skew) + 1 for grade in range(1, number_of + 1)]
    largest = most if full else min(most, max(-(-total // number_of), total * weights[0] // sum(weights)))
    least = 1 if total - largest >= number_of - 1 else 0
    holding, spare = [largest] + [least] * (number_of - 1), total - largest - least * (number_of - 1)
    while spare > 0:
        candidates = [i for i in range(1, number_of) if holding[i] < largest] or [i for i in range(1, number_of) if holding[i] < most]
        mass, remaining = sum([weights[i] for i in candidates]), spare
        for i in candidates:
            addition = min(most - holding[i], max(1, remaining * weights[i] // mass), spare)
            holding[i] = holding[i] + addition
            spare = spare - addition
    return np.array(holding)


def normal_values(rng, dims, spread, most, pieces=(), kind=jnp.bfloat16):
    drawn = spread * jax.random.normal(rng, dims, jnp.float32)
    if pieces:
        drawn = drawn * level_of(rng, dims, pieces, -0.22, 0.18)
    return jnp.clip(drawn, -most, most).astype(kind)


def setup_inputs(seed: int = 0, part: int = 0) -> dict:
    arg_keys = jax.random.split(jax.random.key(seed), 11)
    part_splits = jax.random.split(jax.random.fold_in(arg_keys[10], part), 11)
    tokens = normal_values(part_splits[0], (TOKENS, D), 1.0, 6.0, ((0, 16),))
    expert_ids_keys = jax.random.split(jax.random.fold_in(part_splits[1], 1), TOKENS // TOK_DEV)
    expert_ids_turns = jax.random.permutation(jax.random.fold_in(part_splits[1], 3), TOKENS // TOK_DEV)
    expert_ids = jax.vmap(lambda own, number: assign_block(jax.random.fold_in(part_splits[1], 2), own, number, TOK_DEV, EXPERTS, TOP, CAP, 2))(expert_ids_keys, expert_ids_turns).reshape((TOKENS, TOP))
    gate_probs = jnp.clip(jnp.exp(math.log(0.6) - 2.4849067 * jax.random.uniform(part_splits[2], (TOKENS, TOP), jnp.float32) ** level_of(part_splits[2], (TOKENS, TOP), ((0, 16),), -0.2, 0.2)), 0.05, 0.6)
    w_gate = normal_values(arg_keys[3], (EXPERTS, D, F), D ** -0.5, 0.125, ((0, 16),))
    w_up = normal_values(arg_keys[4], (EXPERTS, D, F), D ** -0.5, 0.125, ((0, 16),))
    w_down = normal_values(arg_keys[5], (EXPERTS, F, D), F ** -0.5, 0.15625, ((0, 16),))
    s_gate = normal_values(arg_keys[6], (D, FS), D ** -0.5, 0.125, ((1, 4),))
    s_up = normal_values(arg_keys[7], (D, FS), D ** -0.5, 0.125, ((1, 4),))
    s_down = normal_values(arg_keys[8], (FS, D), FS ** -0.5, 0.109375, ((0, 4),))
    shared_gate = normal_values(arg_keys[9], (D,), D ** -0.5, 0.125)
    return dict(tokens=tokens, expert_ids=expert_ids, gate_probs=gate_probs, w_gate=w_gate, w_up=w_up, w_down=w_down, s_gate=s_gate, s_up=s_up, s_down=s_down, shared_gate=shared_gate)


def silu_product(rows, w_first, w_second):
    gate = jnp.dot(rows, w_first, preferred_element_type=jnp.float32)
    up = jnp.dot(rows, w_second, preferred_element_type=jnp.float32)
    return (jax.nn.silu(gate) * up).astype(jnp.bfloat16)


def slot_index(ids, experts, capacity):
    flat = ids.reshape(-1).astype(jnp.int32)
    onehot = (flat[:, None] == jnp.arange(experts, dtype=jnp.int32)[None, :]).astype(jnp.int32)
    before = jnp.cumsum(onehot, axis=0) - onehot
    return (flat * capacity + jnp.sum(before * onehot, axis=1)).astype(jnp.int32)


def reference(tokens, expert_ids, gate_probs, w_gate, w_up, w_down, s_gate, s_up, s_down, shared_gate):
    sources = N_EXPERT * N_TENSOR
    blocks = tokens.reshape(sources, TOK_DEV, D)
    slots = jax.vmap(lambda ids: slot_index(ids, EXPERTS, CAP))(expert_ids.reshape(sources, TOK_DEV, TOP))
    repeated = jnp.repeat(blocks, TOP, axis=1)

    def fill(rows, slot):
        return jnp.zeros((EXPERTS * CAP, D), jnp.bfloat16).at[slot].set(rows)

    sent = jax.vmap(fill)(repeated, slots)
    grouped = sent.reshape(sources, EXPERTS, CAP, D).transpose(1, 0, 2, 3).reshape(EXPERTS, sources * CAP, D)

    def run_expert(packed_args):
        rows, first, second, third = packed_args
        hidden = silu_product(rows, first, second)
        return jnp.dot(hidden, third, preferred_element_type=jnp.float32).astype(jnp.bfloat16)

    finished = lax.map(run_expert, (grouped, w_gate, w_up, w_down))
    returned = finished.reshape(EXPERTS, sources, CAP, D).transpose(1, 0, 2, 3).reshape(sources, EXPERTS * CAP, D)
    picked = jax.vmap(lambda outs, slot: outs[slot])(returned, slots).reshape(TOKENS, TOP, D)
    routed = jnp.einsum("tk,tkd->td", gate_probs.astype(jnp.float32), picked.astype(jnp.float32))
    hidden = silu_product(tokens, s_gate, s_up)
    group = FS // N_TENSOR
    shared = jnp.zeros((TOKENS, D), jnp.float32)
    for member in range(N_TENSOR):
        part = jnp.dot(hidden[:, member * group:(member + 1) * group], s_down[member * group:(member + 1) * group], preferred_element_type=jnp.float32)
        shared = shared + part.astype(jnp.bfloat16).astype(jnp.float32)
    scale = jax.nn.sigmoid(jnp.dot(tokens, shared_gate, preferred_element_type=jnp.float32))
    return (scale[:, None] * shared + routed).astype(jnp.bfloat16)
```

```python
import functools

import jax
import jax.numpy as jnp
from jax import lax
from jax.experimental import pallas as pl
from jax.experimental.pallas import tpu as pltpu
from jax.sharding import PartitionSpec as P

MESH = pl.DeviceIdType.MESH
BF = jnp.bfloat16
F32 = jnp.float32


def partner(index, step, size):
    total, bit = 0, 1
    while bit < size:
        total = total + ((index // bit + step // bit) % 2) * bit
        bit *= 2
    return total


def pieces(extent, width):
    return [(start, min(width, extent - start)) for start in range(0, extent, width)]


def layer_kernel(
    ne, nt, cap,
    tok_hbm, ids_ref, prob_ref, wg_hbm, wu_hbm, wd_hbm, sg_hbm, su_hbm, sd_hbm, gate_ref,
    out_ref,
    wg, wu, wd, sg, su, sd,
    meta, meta_z, meta_t,
    tok_t, tok_z, rows, stage, back, back_t, back_z, hidden, hidden_s, part_s, total,
    load_sem, mz_send, mz_recv, mt_send, mt_recv, tz_send, tz_recv, tt_send, tt_recv,
    d_send, d_recv, r_send, r_recv, bt_send, bt_recv, bz_send, bz_recv,
):
    tok, width = out_ref.shape
    top = ids_ref.shape[0]
    experts = ne * nt
    z = lax.axis_index("expert")
    t = lax.axis_index("tensor")

    def remote(src, dst, send, recv, axis, peer):
        return pltpu.make_async_remote_copy(
            src_ref=src, dst_ref=dst, send_sem=send, recv_sem=recv,
            device_id={axis: peer}, device_id_type=MESH,
        )

    def z_peer(s):
        return partner(z, s, ne)

    def t_peer(k):
        return partner(t, k, nt)

    tok_load = pltpu.make_async_copy(tok_hbm, tok_t.at[0], load_sem.at[0])
    tok_load.start()
    barrier = pltpu.get_barrier_semaphore()
    for s in range(1, ne):
        pl.semaphore_signal(barrier, inc=1, device_id={"expert": z_peer(s)}, device_id_type=MESH)
    for k in range(1, nt):
        pl.semaphore_signal(barrier, inc=1, device_id={"tensor": t_peer(k)}, device_id_type=MESH)
    loads = [
        pltpu.make_async_copy(src, dst, load_sem.at[1 + i])
        for i, (src, dst) in enumerate(
            ((sg_hbm, sg), (su_hbm, su), (sd_hbm, sd),
             (wg_hbm.at[0], wg), (wu_hbm.at[0], wu), (wd_hbm.at[0], wd))
        )
    ]

    number = lax.broadcasted_iota(jnp.int32, (experts, tok), 0)
    weight = jnp.zeros((experts, tok), F32)
    chosen = jnp.zeros((experts, tok), F32)
    for k in range(top):
        hit = ids_ref[k:k + 1, :] == number
        weight = weight + jnp.where(hit, prob_ref[k:k + 1, :], 0.0)
        chosen = chosen + jnp.where(hit, 1.0, 0.0)
    earlier = lax.broadcasted_iota(jnp.int32, (tok, tok), 0) < lax.broadcasted_iota(jnp.int32, (tok, tok), 1)
    rank = jnp.dot(chosen.astype(BF), jnp.where(earlier, 1.0, 0.0).astype(BF), preferred_element_type=F32)
    place = jnp.where(chosen > 0.0, rank, -1.0)
    for e in range(ne):
        meta[e, 0:nt, :] = place[e * nt:(e + 1) * nt]
        meta[e, nt:2 * nt, :] = weight[e * nt:(e + 1) * nt]

    def meta_z_copy(s):
        return remote(meta.at[z_peer(s)], meta_z.at[s], mz_send.at[s], mz_recv.at[s], "expert", z_peer(s))

    def meta_t_copy(k):
        return remote(meta.at[z], meta_t.at[k], mt_send.at[k], mt_recv.at[k], "tensor", t_peer(k))

    def tok_z_copy(s):
        return remote(tok_t.at[0], tok_z.at[s], tz_send.at[s], tz_recv.at[s], "expert", z_peer(s))

    def tok_t_copy(k):
        return remote(tok_t.at[0], tok_t.at[k], tt_send.at[k], tt_recv.at[k], "tensor", t_peer(k))

    def dispatch_copy(s, k):
        return remote(
            stage.at[s, pl.ds(k * cap, cap)], rows.at[s, pl.ds(k * cap, cap)],
            d_send.at[s, k], d_recv.at[s, k], "tensor", t_peer(k),
        )

    def return_copy(s, k):
        return remote(
            rows.at[s, pl.ds(k * cap, cap)], back.at[s, pl.ds(k * cap, cap)],
            r_send.at[s, k], r_recv.at[s, k], "tensor", t_peer(k),
        )

    def back_t_copy(k):
        return remote(tok_t.at[k], back_t.at[k], bt_send.at[k], bt_recv.at[k], "tensor", t_peer(k))

    def back_z_copy(s):
        return remote(tok_z.at[s], back_z.at[s], bz_send.at[s], bz_recv.at[s], "expert", z_peer(s))

    tok_load.wait()
    pl.semaphore_wait(barrier, ne - 1 + nt - 1)
    for s in range(1, ne):
        meta_z_copy(s).start()
    for k in range(1, nt):
        meta_t_copy(k).start()
    for s in range(1, ne):
        tok_z_copy(s).start()
    for k in range(1, nt):
        tok_t_copy(k).start()
    for load in loads:
        load.start()
    meta_t[0] = meta[z]

    slots = lax.broadcasted_iota(jnp.int32, (cap, tok), 0).astype(F32)

    def picker(place_row):
        return jnp.where(slots == place_row, 1.0, 0.0).astype(BF)

    def weigher(place_row, weight_row):
        return jnp.where(slots == place_row, weight_row, 0.0).astype(BF)

    def dispatch(s):
        meta_z_copy(s).wait_recv()
        tok_z_copy(s).wait_recv()
        for k in [*range(1, nt), 0]:
            pick = picker(meta_z[s, pl.ds(t_peer(k), 1), :])
            span = pl.ds(k * cap, cap)
            for c, w in pieces(width, 512):
                got = jnp.dot(pick, tok_z[s, :, c:c + w], preferred_element_type=F32).astype(BF)
                if k:
                    stage[s, span, c:c + w] = got
                else:
                    rows[s, span, c:c + w] = got
            if k:
                dispatch_copy(s, k).start()

    def expert(s):
        for c, w in pieces(wg.shape[1], 256):
            x = rows[s]
            g = jnp.dot(x, wg[:, c:c + w], preferred_element_type=F32)
            u = jnp.dot(x, wu[:, c:c + w], preferred_element_type=F32)
            hidden[:, c:c + w] = (g / (1.0 + jnp.exp(-g)) * u).astype(BF)
        for c, w in pieces(width, 256):
            rows[s, :, c:c + w] = jnp.dot(hidden[...], wd[:, c:c + w], preferred_element_type=F32).astype(BF)

    def each(first, last, body):
        def step(i, carry):
            body(i)
            return carry
        lax.fori_loop(first, last, step, 0)

    early = min(ne, ne // 2 + 1)
    each(1, early, dispatch)

    for k in range(1, nt):
        tok_t_copy(k).wait_recv()
        meta_t_copy(k).wait_recv()
    for load in loads[:3]:
        load.wait()
    nk = (((1,), (1,)), ((), ()))
    all_rows = nt * tok
    for c, w in pieces(sg.shape[0], 256):
        x = tok_t[...].reshape(all_rows, width)
        g = lax.dot_general(x, sg[c:c + w, :], nk, preferred_element_type=F32)
        u = lax.dot_general(x, su[c:c + w, :], nk, preferred_element_type=F32)
        hidden_s[:, c:c + w] = (g / (1.0 + jnp.exp(-g)) * u).astype(BF)
    for c, w in pieces(width, 256):
        part_s[:, c:c + w] = jnp.dot(hidden_s[...], sd[:, c:c + w], preferred_element_type=F32).astype(BF)

    each(early, ne, dispatch)

    for load in loads[3:]:
        load.wait()
    for k in range(nt):
        pick = picker(meta_t[k, pl.ds(t, 1), :])
        for c, w in pieces(width, 512):
            rows[0, k * cap:(k + 1) * cap, c:c + w] = jnp.dot(
                pick, tok_t[k, :, c:c + w], preferred_element_type=F32).astype(BF)

    def routed_stage(i):
        s = (i + 1) % (ne - 1) + 1 if ne > 2 else i + 1
        s = jnp.where(i == ne - 1, 0, s)
        last = i == ne - 1

        @pl.when(jnp.logical_not(last))
        def _():
            for k in range(1, nt):
                dispatch_copy(s, k).wait_recv()

        expert(s)

        @pl.when(jnp.logical_not(last))
        def _():
            for k in range(1, nt):
                return_copy(s, k).start()
            back[s, 0:cap] = rows[s, 0:cap]

    each(0, ne, routed_stage)

    flip = (((0,), (0,)), ((), ()))
    for k in range(1, nt):
        tok_t_copy(k).wait_send()
    for s in range(1, ne):
        tok_z_copy(s).wait_send()
    for k in [*range(1, nt), 0]:
        part = weigher(meta_t[k, pl.ds(t, 1), :], meta_t[k, pl.ds(nt + t, 1), :])
        logit = jnp.sum(tok_t[k].astype(F32) * gate_ref[...].astype(F32), axis=1, keepdims=True)
        scale = 1.0 / (1.0 + jnp.exp(-logit))
        for c, w in pieces(width, 512):
            got = lax.dot_general(part, rows[0, k * cap:(k + 1) * cap, c:c + w], flip, preferred_element_type=F32)
            got = got + scale * part_s[k * tok:(k + 1) * tok, c:c + w].astype(F32)
            if k:
                tok_t[k, :, c:c + w] = got.astype(BF)
            else:
                total[:, c:c + w] = got
        if k:
            back_t_copy(k).start()

    def combine(i):
        s = (i + 1) % (ne - 1) + 1 if ne > 2 else i + 1
        for k in range(1, nt):
            return_copy(s, k).wait_recv()
        parts = jnp.concatenate(
            [weigher(meta_z[s, pl.ds(t_peer(k), 1), :], meta_z[s, pl.ds(nt + t_peer(k), 1), :]) for k in range(nt)],
            axis=0,
        )
        for c, w in pieces(width, 512):
            tok_z[s, :, c:c + w] = lax.dot_general(
                parts, back[s, :, c:c + w], flip, preferred_element_type=F32).astype(BF)
        back_z_copy(s).start()

    each(0, ne - 1, combine)
    for s in range(1, ne):
        back_z_copy(s).wait_recv()
        total[...] += back_z[s].astype(F32)
    for k in range(1, nt):
        back_t_copy(k).wait_recv()
        total[...] += back_t[k].astype(F32)
    out_ref[...] = total[...].astype(BF)

    for s in range(1, ne):
        meta_z_copy(s).wait_send()
        back_z_copy(s).wait_send()
        for k in range(1, nt):
            dispatch_copy(s, k).wait_send()
            return_copy(s, k).wait_send()
    for k in range(1, nt):
        meta_t_copy(k).wait_send()
        back_t_copy(k).wait_send()


def per_device(
    tokens, expert_ids, gate_probs, w_gate, w_up, w_down, s_gate, s_up, s_down, shared_gate
):
    tok, width = tokens.shape
    top = expert_ids.shape[1]
    ne = lax.axis_size("expert")
    nt = lax.axis_size("tensor")
    experts = ne * nt
    cap = max(2, 2 * top * tok // experts)
    inner = w_gate.shape[2]
    inner_s = s_gate.shape[1]
    vmem = pl.BlockSpec(memory_space=pltpu.VMEM)
    hbm = pl.BlockSpec(memory_space=pl.ANY)
    dma = pltpu.SemaphoreType.DMA
    group = nt * cap
    return pl.pallas_call(
        functools.partial(layer_kernel, ne, nt, cap),
        out_shape=jax.ShapeDtypeStruct((tok, width), BF),
        in_specs=[hbm, vmem, vmem, hbm, hbm, hbm, hbm, hbm, hbm, vmem],
        out_specs=vmem,
        scratch_shapes=[
            pltpu.VMEM((width, inner), BF),
            pltpu.VMEM((width, inner), BF),
            pltpu.VMEM((inner, width), BF),
            pltpu.VMEM((inner_s, width), BF),
            pltpu.VMEM((inner_s, width), BF),
            pltpu.VMEM((inner_s, width), BF),
            pltpu.VMEM((ne, 2 * nt, tok), F32),
            pltpu.VMEM((ne, 2 * nt, tok), F32),
            pltpu.VMEM((nt, 2 * nt, tok), F32),
            pltpu.VMEM((nt, tok, width), BF),
            pltpu.VMEM((ne, tok, width), BF),
            pltpu.VMEM((ne, group, width), BF),
            pltpu.VMEM((ne, group, width), BF),
            pltpu.VMEM((ne, group, width), BF),
            pltpu.VMEM((nt, tok, width), BF),
            pltpu.VMEM((ne, tok, width), BF),
            pltpu.VMEM((group, inner), BF),
            pltpu.VMEM((nt * tok, inner_s), BF),
            pltpu.VMEM((nt * tok, width), BF),
            pltpu.VMEM((tok, width), F32),
            dma((7,)),
            dma((ne,)), dma((ne,)), dma((nt,)), dma((nt,)),
            dma((ne,)), dma((ne,)), dma((nt,)), dma((nt,)),
            dma((ne, nt)), dma((ne, nt)), dma((ne, nt)), dma((ne, nt)),
            dma((nt,)), dma((nt,)), dma((ne,)), dma((ne,)),
        ],
        compiler_params=pltpu.CompilerParams(
            collective_id=0, has_side_effects=True, vmem_limit_bytes=67043328
        ),
        name="moe_layer",
    )(
        tokens, expert_ids.T, gate_probs.T, w_gate, w_up, w_down,
        s_gate.T, s_up.T, s_down, shared_gate.reshape(1, width),
    )


def solution(mesh):
    return jax.shard_map(
        per_device,
        mesh=mesh,
        in_specs=(
            P(("dp", "expert", "tensor"), None),
            P(("dp", "expert", "tensor"), None),
            P(("dp", "expert", "tensor"), None),
            P(("expert", "tensor"), None, None),
            P(("expert", "tensor"), None, None),
            P(("expert", "tensor"), None, None),
            P(None, "tensor"),
            P(None, "tensor"),
            P("tensor", None),
            P(),
        ),
        out_specs=P(("dp", "expert", "tensor"), None),
        check_vma=False,
    )
```

```python
import functools

import jax
import jax.numpy as jnp
from jax import lax
from jax.experimental import pallas as pl
from jax.experimental.pallas import tpu as pltpu
from jax.sharding import PartitionSpec as P

MESH = pl.DeviceIdType.MESH
BF = jnp.bfloat16
F32 = jnp.float32


def partner(index, step, size):
    total, bit = 0, 1
    while bit < size:
        total = total + ((index // bit + step // bit) % 2) * bit
        bit *= 2
    return total


def pieces(extent, width):
    return [(start, min(width, extent - start)) for start in range(0, extent, width)]


def layer_kernel(
    ne, nt, cap,
    tok_hbm, ids_ref, prob_ref, wg_hbm, wu_hbm, wd_hbm, sg_hbm, su_hbm, sd_hbm, gate_ref,
    out_ref,
    wg, wu, wd, sg, su, sd,
    meta, meta_z, meta_t,
    tok_t, tok_z, rows, stage, back, back_t, back_z, hidden, hidden_s, part_s, total, held,
    load_sem, mz_send, mz_recv, mt_send, mt_recv, tz_send, tz_recv, tt_send, tt_recv,
    d_send, d_recv, r_send, r_recv, bt_send, bt_recv, bz_send, bz_recv,
):
    tok, width = out_ref.shape
    top = ids_ref.shape[0]
    experts = ne * nt
    z = lax.axis_index("expert")
    t = lax.axis_index("tensor")

    def remote(src, dst, send, recv, axis, peer):
        return pltpu.make_async_remote_copy(
            src_ref=src, dst_ref=dst, send_sem=send, recv_sem=recv,
            device_id={axis: peer}, device_id_type=MESH,
        )

    def z_peer(s):
        return partner(z, s, ne)

    def t_peer(k):
        return partner(t, k, nt)

    tok_load = pltpu.make_async_copy(tok_hbm, tok_t.at[0], load_sem.at[0])
    tok_load.start()
    barrier = pltpu.get_barrier_semaphore()
    for s in range(1, ne):
        pl.semaphore_signal(barrier, inc=1, device_id={"expert": z_peer(s)}, device_id_type=MESH)
    for k in range(1, nt):
        pl.semaphore_signal(barrier, inc=1, device_id={"tensor": t_peer(k)}, device_id_type=MESH)
    loads = [
        pltpu.make_async_copy(src, dst, load_sem.at[1 + i])
        for i, (src, dst) in enumerate(
            ((sg_hbm, sg), (su_hbm, su), (sd_hbm, sd),
             (wg_hbm.at[0], wg), (wu_hbm.at[0], wu), (wd_hbm.at[0], wd))
        )
    ]

    number = lax.broadcasted_iota(jnp.int32, (experts, tok), 0)
    weight = jnp.zeros((experts, tok), F32)
    chosen = jnp.zeros((experts, tok), F32)
    for k in range(top):
        hit = ids_ref[k:k + 1, :] == number
        weight = weight + jnp.where(hit, prob_ref[k:k + 1, :], 0.0)
        chosen = chosen + jnp.where(hit, 1.0, 0.0)
    earlier = lax.broadcasted_iota(jnp.int32, (tok, tok), 0) < lax.broadcasted_iota(jnp.int32, (tok, tok), 1)
    rank = jnp.dot(chosen.astype(BF), jnp.where(earlier, 1.0, 0.0).astype(BF), preferred_element_type=F32)
    place = jnp.where(chosen > 0.0, rank, -1.0)
    for e in range(ne):
        meta[e, 0:nt, :] = place[e * nt:(e + 1) * nt]
        meta[e, nt:2 * nt, :] = weight[e * nt:(e + 1) * nt]

    def meta_z_copy(s):
        return remote(meta.at[z_peer(s)], meta_z.at[s], mz_send.at[s], mz_recv.at[s], "expert", z_peer(s))

    def meta_t_copy(k):
        return remote(meta, meta_t.at[k], mt_send.at[k], mt_recv.at[k], "tensor", t_peer(k))

    def tok_z_copy(s):
        return remote(tok_t.at[0], tok_z.at[s], tz_send.at[s], tz_recv.at[s], "expert", z_peer(s))

    def forward_copy(s):
        return remote(tok_z.at[s - 1], tok_z.at[s], tz_send.at[s], tz_recv.at[s], "expert", z_peer(1))

    half = tok // 2
    relayed = nt == 4

    def part_rows(h):
        return pl.ds(h * half, half)

    def tok_t_copy(k, h):
        return remote(
            tok_t.at[0, part_rows(h)], tok_t.at[k, part_rows(h)],
            tt_send.at[k, h], tt_recv.at[k, h], "tensor", t_peer(k),
        )

    def relay_copy(h):
        return remote(
            tok_t.at[2 - h, part_rows(h)], tok_t.at[3, part_rows(h)],
            tt_send.at[3, h], tt_recv.at[3, h], "tensor", t_peer(1 + h),
        )

    def near_copy(k):
        return remote(
            stage.at[1, pl.ds(k * cap, cap)], rows.at[1, pl.ds(k * cap, cap)],
            d_send.at[1, k], d_recv.at[1, k], "expert", z_peer(1),
        )

    def near_back_copy():
        return remote(rows.at[1], back.at[1], r_send.at[1, 0], r_recv.at[1, 0], "expert", z_peer(1))

    def dispatch_copy(s, k):
        return remote(
            stage.at[s, pl.ds(k * cap, cap)], rows.at[s, pl.ds(k * cap, cap)],
            d_send.at[s, k], d_recv.at[s, k], "tensor", t_peer(k),
        )

    def return_copy(s, k):
        return remote(
            rows.at[s, pl.ds(k * cap, cap)], back.at[s, pl.ds(k * cap, cap)],
            r_send.at[s, k], r_recv.at[s, k], "tensor", t_peer(k),
        )

    def back_t_copy(k, h):
        return remote(
            tok_t.at[k, part_rows(h)], back_t.at[k, part_rows(h)],
            bt_send.at[k, h], bt_recv.at[k, h], "tensor", t_peer(k),
        )

    def back_relay_copy(h):
        return remote(
            tok_t.at[3, part_rows(h)], back_t.at[3, part_rows(h)],
            bt_send.at[3, h], bt_recv.at[3, h], "tensor", t_peer(1 + h),
        )

    def back_z_copy(s):
        return remote(tok_z.at[s], back_z.at[s], bz_send.at[s], bz_recv.at[s], "expert", z_peer(s))

    def back_near_copy(s):
        return remote(tok_z.at[s], back_z.at[s], bz_send.at[s], bz_recv.at[s], "expert", z_peer(1))

    def each(first, last, body):
        def step(i, carry):
            body(i)
            return carry
        lax.fori_loop(first, last, step, 0)

    direct = [(2, 0), (1, 1), (2, 1), (1, 0)] if relayed else [(k, h) for k in range(1, nt) for h in range(2)]
    peers = sorted({k for k, _ in direct})

    tok_load.wait()
    pl.semaphore_wait(barrier, ne - 1 + nt - 1)
    for k, h in direct:
        tok_t_copy(k, h).start()
    for s in range(2, ne, 2):
        tok_z_copy(s).start()
    for k in range(1, nt):
        meta_t_copy(k).start()
    for s in range(2, ne):
        meta_z_copy(s).start()
    for load in loads:
        load.start()
    meta_t[0] = meta[...]

    slots = lax.broadcasted_iota(jnp.int32, (cap, tok), 0).astype(F32)

    def picker(place_row):
        return jnp.where(slots == place_row, 1.0, 0.0).astype(BF)

    def weigher(place_row, weight_row):
        return jnp.where(slots == place_row, weight_row, 0.0).astype(BF)

    def near(k):
        pick = picker(meta_t[k, z_peer(1), pl.ds(t, 1), :])
        for c, w in pieces(width, 512):
            stage[1, k * cap:(k + 1) * cap, c:c + w] = jnp.dot(
                pick, tok_t[k, :, c:c + w], preferred_element_type=F32).astype(BF)
        near_copy(k).start()

    def dispatch(s):
        for k in [*range(1, nt), 0]:
            pick = picker(meta_z[s, pl.ds(t_peer(k), 1), :])
            span = pl.ds(k * cap, cap)
            for c, w in pieces(width, 512):
                got = jnp.dot(pick, tok_z[s, :, c:c + w], preferred_element_type=F32).astype(BF)
                if k:
                    stage[s, span, c:c + w] = got
                else:
                    rows[s, span, c:c + w] = got
            if k:
                dispatch_copy(s, k).start()

    def dispatch_even(j):
        s = 2 * j
        tok_z_copy(s).wait_recv()
        forward_copy(s + 1).start()
        meta_z_copy(s).wait_recv()
        dispatch(s)

    def dispatch_odd(j):
        s = 2 * j + 1
        forward_copy(s).wait_recv()
        meta_z_copy(s).wait_recv()
        dispatch(s)

    def expert(s):
        for c, w in pieces(wg.shape[1], 256):
            x = rows[s]
            g = jnp.dot(x, wg[:, c:c + w], preferred_element_type=F32)
            u = jnp.dot(x, wu[:, c:c + w], preferred_element_type=F32)
            hidden[:, c:c + w] = (g / (1.0 + jnp.exp(-g)) * u).astype(BF)
        for c, w in pieces(width, 256):
            rows[s, :, c:c + w] = jnp.dot(hidden[...], wd[:, c:c + w], preferred_element_type=F32).astype(BF)

    near(0)
    if relayed:
        tok_t_copy(2, 0).wait_recv()
        relay_copy(0).start()
        tok_t_copy(1, 1).wait_recv()
        relay_copy(1).start()
        rest = [(2, 1), (1, 0)]
    else:
        rest = direct
    for k, h in rest:
        tok_t_copy(k, h).wait_recv()
    for k in range(1, nt):
        meta_t_copy(k).wait_recv()
    for k in peers:
        near(k)
    each(1, ne // 2, dispatch_even)
    if relayed:
        for h in range(2):
            relay_copy(h).wait_recv()
        near(3)

    for load in loads[:3]:
        load.wait()
    nk = (((1,), (1,)), ((), ()))
    all_rows = nt * tok
    for c, w in pieces(sg.shape[0], 256):
        x = tok_t[...].reshape(all_rows, width)
        g = lax.dot_general(x, sg[c:c + w, :], nk, preferred_element_type=F32)
        u = lax.dot_general(x, su[c:c + w, :], nk, preferred_element_type=F32)
        hidden_s[:, c:c + w] = (g / (1.0 + jnp.exp(-g)) * u).astype(BF)

    each(1, ne // 2, dispatch_odd)

    for c, w in pieces(width, 256):
        part_s[:, c:c + w] = jnp.dot(hidden_s[...], sd[:, c:c + w], preferred_element_type=F32).astype(BF)

    for load in loads[3:]:
        load.wait()
    for k in range(nt):
        pick = picker(meta_t[k, z, pl.ds(t, 1), :])
        for c, w in pieces(width, 512):
            rows[0, k * cap:(k + 1) * cap, c:c + w] = jnp.dot(
                pick, tok_t[k, :, c:c + w], preferred_element_type=F32).astype(BF)

    def routed_stage(i):
        pairs = ne // 2
        s = jnp.where(i < pairs - 1, 2 * i + 2, 2 * (i - pairs) + 3)
        s = jnp.where(i == pairs - 1, 1, s)
        s = jnp.where(i == ne - 1, 0, s)

        @pl.when(s == 1)
        def _():
            for k in range(nt):
                near_copy(k).wait_recv()

        @pl.when(s > 1)
        def _():
            for k in range(1, nt):
                dispatch_copy(s, k).wait_recv()

        expert(s)

        @pl.when(s == 1)
        def _():
            near_back_copy().start()

        @pl.when(s > 1)
        def _():
            for k in range(1, nt):
                return_copy(s, k).start()
            back[s, 0:cap] = rows[s, 0:cap]

    each(0, ne, routed_stage)

    flip = (((0,), (0,)), ((), ()))

    def combined(s):
        for k in range(1, nt):
            return_copy(s, k).wait_recv()
        return jnp.concatenate(
            [weigher(meta_z[s, pl.ds(t_peer(k), 1), :], meta_z[s, pl.ds(nt + t_peer(k), 1), :]) for k in range(nt)],
            axis=0,
        )

    def combine_odd(j):
        s = 2 * j + 1
        parts = combined(s)
        for c, w in pieces(width, 512):
            tok_z[s, :, c:c + w] = lax.dot_general(
                parts, back[s, :, c:c + w], flip, preferred_element_type=F32).astype(BF)
        back_near_copy(s).start()

    def combine_even(j):
        s = 2 * j
        parts = combined(s)
        forward_copy(s + 1).wait_send()
        back_near_copy(s + 1).wait_recv()
        for c, w in pieces(width, 512):
            got = lax.dot_general(parts, back[s, :, c:c + w], flip, preferred_element_type=F32)
            tok_z[s, :, c:c + w] = (got + back_z[s + 1, :, c:c + w].astype(F32)).astype(BF)
        back_z_copy(s).start()

    each(1, ne // 2, combine_odd)

    for k, h in direct:
        tok_t_copy(k, h).wait_send()
    if relayed:
        for h in range(2):
            relay_copy(h).wait_send()
    near_back_copy().wait_recv()

    for k in ([3, 1, 2, 0] if relayed else [*range(1, nt), 0]):
        own = weigher(meta_t[k, z, pl.ds(t, 1), :], meta_t[k, z, pl.ds(nt + t, 1), :])
        by = z_peer(1)
        other = weigher(meta_t[k, by, pl.ds(t, 1), :], meta_t[k, by, pl.ds(nt + t, 1), :])
        logit = jnp.sum(tok_t[k].astype(F32) * gate_ref[...].astype(F32), axis=1, keepdims=True)
        scale = 1.0 / (1.0 + jnp.exp(-logit))
        span = slice(k * cap, (k + 1) * cap)
        for c, w in pieces(width, 512):
            got = lax.dot_general(own, rows[0, span, c:c + w], flip, preferred_element_type=F32)
            got = got + lax.dot_general(other, back[1, span, c:c + w], flip, preferred_element_type=F32)
            got = got + scale * part_s[k * tok:(k + 1) * tok, c:c + w].astype(F32)
            if k == 0:
                total[:, c:c + w] = got
            elif relayed and k < 3:
                now = slice((1 - k % 2) * half, (2 - k % 2) * half)
                later = slice((k % 2) * half, (k % 2 + 1) * half)
                tok_t[k, now, c:c + w] = got[now].astype(BF)
                held[k, :, c:c + w] = got[later]
            else:
                tok_t[k, :, c:c + w] = got.astype(BF)
        if relayed and k == 3:
            for h in range(2):
                back_relay_copy(h).start()
        elif relayed and k:
            back_t_copy(k, 1 - k % 2).start()
        elif k:
            for h in range(2):
                back_t_copy(k, h).start()
    if relayed:
        for k in (1, 2):
            h = k % 2
            back_relay_copy(h).wait_recv()
            tok_t[k, part_rows(h), :] = (held[k] + back_t[3, part_rows(h), :].astype(F32)).astype(BF)
            back_t_copy(k, h).start()

    each(1, ne // 2, combine_even)

    for k in peers:
        for h in range(2):
            back_t_copy(k, h).wait_recv()
        total[...] += back_t[k].astype(F32)
    for s in range(2, ne, 2):
        back_z_copy(s).wait_recv()
        total[...] += back_z[s].astype(F32)
    out_ref[...] = total[...].astype(BF)

    for k in range(nt):
        near_copy(k).wait_send()
    near_back_copy().wait_send()
    for s in range(2, ne):
        meta_z_copy(s).wait_send()
        for k in range(1, nt):
            dispatch_copy(s, k).wait_send()
            return_copy(s, k).wait_send()
    for s in range(2, ne, 2):
        tok_z_copy(s).wait_send()
        back_z_copy(s).wait_send()
        back_near_copy(s + 1).wait_send()
    for k in range(1, nt):
        meta_t_copy(k).wait_send()
    for k, h in direct:
        back_t_copy(k, h).wait_send()
    if relayed:
        for h in range(2):
            back_relay_copy(h).wait_send()


def per_device(
    tokens, expert_ids, gate_probs, w_gate, w_up, w_down, s_gate, s_up, s_down, shared_gate
):
    tok, width = tokens.shape
    top = expert_ids.shape[1]
    ne = lax.axis_size("expert")
    nt = lax.axis_size("tensor")
    experts = ne * nt
    cap = max(2, 2 * top * tok // experts)
    inner = w_gate.shape[2]
    inner_s = s_gate.shape[1]
    vmem = pl.BlockSpec(memory_space=pltpu.VMEM)
    hbm = pl.BlockSpec(memory_space=pl.ANY)
    dma = pltpu.SemaphoreType.DMA
    group = nt * cap
    return pl.pallas_call(
        functools.partial(layer_kernel, ne, nt, cap),
        out_shape=jax.ShapeDtypeStruct((tok, width), BF),
        in_specs=[hbm, vmem, vmem, hbm, hbm, hbm, hbm, hbm, hbm, vmem],
        out_specs=vmem,
        scratch_shapes=[
            pltpu.VMEM((width, inner), BF),
            pltpu.VMEM((width, inner), BF),
            pltpu.VMEM((inner, width), BF),
            pltpu.VMEM((inner_s, width), BF),
            pltpu.VMEM((inner_s, width), BF),
            pltpu.VMEM((inner_s, width), BF),
            pltpu.VMEM((ne, 2 * nt, tok), F32),
            pltpu.VMEM((ne, 2 * nt, tok), F32),
            pltpu.VMEM((nt, ne, 2 * nt, tok), F32),
            pltpu.VMEM((nt, tok, width), BF),
            pltpu.VMEM((ne, tok, width), BF),
            pltpu.VMEM((ne, group, width), BF),
            pltpu.VMEM((ne, group, width), BF),
            pltpu.VMEM((ne, group, width), BF),
            pltpu.VMEM((nt, tok, width), BF),
            pltpu.VMEM((ne, tok, width), BF),
            pltpu.VMEM((group, inner), BF),
            pltpu.VMEM((nt * tok, inner_s), BF),
            pltpu.VMEM((nt * tok, width), BF),
            pltpu.VMEM((tok, width), F32),
            pltpu.VMEM((3, tok // 2, width), F32),
            dma((7,)),
            dma((ne,)), dma((ne,)), dma((nt,)), dma((nt,)),
            dma((ne,)), dma((ne,)), dma((nt, 2)), dma((nt, 2)),
            dma((ne, nt)), dma((ne, nt)), dma((ne, nt)), dma((ne, nt)),
            dma((nt, 2)), dma((nt, 2)), dma((ne,)), dma((ne,)),
        ],
        compiler_params=pltpu.CompilerParams(
            collective_id=0, has_side_effects=True, vmem_limit_bytes=67043328
        ),
        name="moe_layer",
    )(
        tokens, expert_ids.T, gate_probs.T, w_gate, w_up, w_down,
        s_gate.T, s_up.T, s_down, shared_gate.reshape(1, width),
    )


def solution(mesh):
    return jax.shard_map(
        per_device,
        mesh=mesh,
        in_specs=(
            P(("dp", "expert", "tensor"), None),
            P(("dp", "expert", "tensor"), None),
            P(("dp", "expert", "tensor"), None),
            P(("expert", "tensor"), None, None),
            P(("expert", "tensor"), None, None),
            P(("expert", "tensor"), None, None),
            P(None, "tensor"),
            P(None, "tensor"),
            P("tensor", None),
            P(),
        ),
        out_specs=P(("dp", "expert", "tensor"), None),
        check_vma=False,
    )
```

```python
import functools

import jax
import jax.numpy as jnp
from jax import lax
from jax.experimental import pallas as pl
from jax.experimental.pallas import tpu as pltpu
from jax.sharding import PartitionSpec as P

MESH = pl.DeviceIdType.MESH
BF = jnp.bfloat16
F32 = jnp.float32


def partner(index, step, size):
    total, bit = 0, 1
    while bit < size:
        total = total + ((index // bit + step // bit) % 2) * bit
        bit *= 2
    return total


def pieces(extent, width):
    return [(start, min(width, extent - start)) for start in range(0, extent, width)]


def layer_kernel(
    ne, nt, cap,
    tok_hbm, ids_ref, prob_ref, wg_hbm, wu_hbm, wd_hbm, sg_hbm, su_hbm, sd_hbm, gate_ref,
    out_ref,
    wg, wu, wd, sg, su, sd,
    meta, meta_z, meta_t,
    tok_t, tok_z, rows, stage, back, back_t, back_z, hidden, hidden_s, part_s, total, held,
    load_sem, mz_send, mz_recv, mt_send, mt_recv, tz_send, tz_recv, tt_send, tt_recv,
    d_send, d_recv, r_send, r_recv, bt_send, bt_recv, bz_send, bz_recv,
):
    tok, width = out_ref.shape
    top = ids_ref.shape[0]
    experts = ne * nt
    z = lax.axis_index("expert")
    t = lax.axis_index("tensor")

    def remote(src, dst, send, recv, axis, peer):
        return pltpu.make_async_remote_copy(
            src_ref=src, dst_ref=dst, send_sem=send, recv_sem=recv,
            device_id={axis: peer}, device_id_type=MESH,
        )

    def z_peer(s):
        return partner(z, s, ne)

    def t_peer(k):
        return partner(t, k, nt)

    tok_load = pltpu.make_async_copy(tok_hbm, tok_t.at[0], load_sem.at[0])
    tok_load.start()
    barrier = pltpu.get_barrier_semaphore()
    for s in range(1, ne):
        pl.semaphore_signal(barrier, inc=1, device_id={"expert": z_peer(s)}, device_id_type=MESH)
    for k in range(1, nt):
        pl.semaphore_signal(barrier, inc=1, device_id={"tensor": t_peer(k)}, device_id_type=MESH)
    loads = [
        pltpu.make_async_copy(src, dst, load_sem.at[1 + i])
        for i, (src, dst) in enumerate(
            ((sg_hbm, sg), (su_hbm, su), (sd_hbm, sd),
             (wg_hbm.at[0], wg), (wu_hbm.at[0], wu), (wd_hbm.at[0], wd))
        )
    ]

    number = lax.broadcasted_iota(jnp.int32, (experts, tok), 0)
    weight = jnp.zeros((experts, tok), F32)
    chosen = jnp.zeros((experts, tok), F32)
    for k in range(top):
        hit = ids_ref[k:k + 1, :] == number
        weight = weight + jnp.where(hit, prob_ref[k:k + 1, :], 0.0)
        chosen = chosen + jnp.where(hit, 1.0, 0.0)
    earlier = lax.broadcasted_iota(jnp.int32, (tok, tok), 0) < lax.broadcasted_iota(jnp.int32, (tok, tok), 1)
    rank = jnp.dot(chosen.astype(BF), jnp.where(earlier, 1.0, 0.0).astype(BF), preferred_element_type=F32)
    place = jnp.where(chosen > 0.0, rank, -1.0)
    for e in range(ne):
        meta[e, 0:nt, :] = place[e * nt:(e + 1) * nt]
        meta[e, nt:2 * nt, :] = weight[e * nt:(e + 1) * nt]

    def meta_z_copy(s):
        return remote(meta.at[z_peer(s)], meta_z.at[s], mz_send.at[s], mz_recv.at[s], "expert", z_peer(s))

    def meta_t_copy(k):
        return remote(meta, meta_t.at[k], mt_send.at[k], mt_recv.at[k], "tensor", t_peer(k))

    def tok_z_copy(s):
        return remote(tok_t.at[0], tok_z.at[s], tz_send.at[s], tz_recv.at[s], "expert", z_peer(s))

    def forward_copy(s):
        return remote(tok_z.at[s - 1], tok_z.at[s], tz_send.at[s], tz_recv.at[s], "expert", z_peer(1))

    half = tok // 2
    relayed = nt == 4

    def part_rows(h):
        return pl.ds(h * half, half)

    def tok_t_copy(k, h):
        return remote(
            tok_t.at[0, part_rows(h)], tok_t.at[k, part_rows(h)],
            tt_send.at[k, h], tt_recv.at[k, h], "tensor", t_peer(k),
        )

    def relay_copy(h):
        return remote(
            tok_t.at[2 - h, part_rows(h)], tok_t.at[3, part_rows(h)],
            tt_send.at[3, h], tt_recv.at[3, h], "tensor", t_peer(1 + h),
        )

    def near_back_copy():
        return remote(rows.at[1], back.at[1], r_send.at[1, 0], r_recv.at[1, 0], "expert", z_peer(1))

    def dispatch_copy(s, k):
        return remote(
            stage.at[s, pl.ds(k * cap, cap)], rows.at[s, pl.ds(k * cap, cap)],
            d_send.at[s, k], d_recv.at[s, k], "tensor", t_peer(k),
        )

    def return_copy(s, k):
        return remote(
            rows.at[s, pl.ds(k * cap, cap)], back.at[s, pl.ds(k * cap, cap)],
            r_send.at[s, k], r_recv.at[s, k], "tensor", t_peer(k),
        )

    def back_t_copy(k, h):
        return remote(
            tok_t.at[k, part_rows(h)], back_t.at[k, part_rows(h)],
            bt_send.at[k, h], bt_recv.at[k, h], "tensor", t_peer(k),
        )

    def back_relay_copy(h):
        return remote(
            tok_t.at[3, part_rows(h)], back_t.at[3, part_rows(h)],
            bt_send.at[3, h], bt_recv.at[3, h], "tensor", t_peer(1 + h),
        )

    def columns(h):
        return pl.ds(h * (width // 2), width // 2)

    def back_z_copy(s, h):
        return remote(
            tok_z.at[s, :, columns(h)], back_z.at[s, :, columns(h)],
            bz_send.at[s, h], bz_recv.at[s, h], "expert", z_peer(s),
        )

    def back_near_copy(s, h):
        return remote(
            tok_z.at[s, :, columns(h)], back_z.at[s, :, columns(h)],
            bz_send.at[s, h], bz_recv.at[s, h], "expert", z_peer(1),
        )

    def each(first, last, body):
        def step(i, carry):
            body(i)
            return carry
        lax.fori_loop(first, last, step, 0)

    direct = [(2, 0), (1, 1), (2, 1), (1, 0)] if relayed else [(k, h) for k in range(1, nt) for h in range(2)]
    peers = sorted({k for k, _ in direct})

    own_steps = [s for s in range(1, ne) if s == 1 or s % 2 == 0]

    tok_load.wait()
    pl.semaphore_wait(barrier, ne - 1 + nt - 1)
    for k, h in direct:
        tok_t_copy(k, h).start()
    for s in own_steps:
        tok_z_copy(s).start()
    for k in range(1, nt):
        meta_t_copy(k).start()
    for s in range(1, ne):
        meta_z_copy(s).start()
    for load in loads:
        load.start()
    meta_t[0] = meta[...]

    slots = lax.broadcasted_iota(jnp.int32, (cap, tok), 0).astype(F32)

    def picker(place_row):
        return jnp.where(slots == place_row, 1.0, 0.0).astype(BF)

    def weigher(place_row, weight_row):
        return jnp.where(slots == place_row, weight_row, 0.0).astype(BF)

    def dispatch(s):
        for k in [*range(1, nt), 0]:
            pick = picker(meta_z[s, pl.ds(t_peer(k), 1), :])
            span = pl.ds(k * cap, cap)
            for c, w in pieces(width, 512):
                got = jnp.dot(pick, tok_z[s, :, c:c + w], preferred_element_type=F32).astype(BF)
                if k:
                    stage[s, span, c:c + w] = got
                else:
                    rows[s, span, c:c + w] = got
            if k:
                dispatch_copy(s, k).start()

    def dispatch_even(j):
        s = 2 * j
        tok_z_copy(s).wait_recv()
        forward_copy(s + 1).start()
        meta_z_copy(s).wait_recv()
        dispatch(s)

    def dispatch_odd(j):
        s = 2 * j + 1
        forward_copy(s).wait_recv()
        meta_z_copy(s).wait_recv()
        dispatch(s)

    def expert(s):
        for c, w in pieces(wg.shape[1], 256):
            x = rows[s]
            g = jnp.dot(x, wg[:, c:c + w], preferred_element_type=F32)
            u = jnp.dot(x, wu[:, c:c + w], preferred_element_type=F32)
            hidden[:, c:c + w] = (g / (1.0 + jnp.exp(-g)) * u).astype(BF)
        for c, w in pieces(width, 256):
            rows[s, :, c:c + w] = jnp.dot(hidden[...], wd[:, c:c + w], preferred_element_type=F32).astype(BF)

    if relayed:
        tok_t_copy(2, 0).wait_recv()
        relay_copy(0).start()
        tok_t_copy(1, 1).wait_recv()
        relay_copy(1).start()
        rest = [(2, 1), (1, 0)]
    else:
        rest = direct
    tok_z_copy(1).wait_recv()
    meta_z_copy(1).wait_recv()
    dispatch(1)
    for k, h in rest:
        tok_t_copy(k, h).wait_recv()
    for k in range(1, nt):
        meta_t_copy(k).wait_recv()
    if relayed:
        for h in range(2):
            relay_copy(h).wait_recv()

    for load in loads[:3]:
        load.wait()
    nk = (((1,), (1,)), ((), ()))
    all_rows = nt * tok
    for c, w in pieces(sg.shape[0], 256):
        x = tok_t[...].reshape(all_rows, width)
        g = lax.dot_general(x, sg[c:c + w, :], nk, preferred_element_type=F32)
        u = lax.dot_general(x, su[c:c + w, :], nk, preferred_element_type=F32)
        hidden_s[:, c:c + w] = (g / (1.0 + jnp.exp(-g)) * u).astype(BF)

    each(1, ne // 2, dispatch_even)

    for c, w in pieces(width, 256):
        part_s[:, c:c + w] = jnp.dot(hidden_s[...], sd[:, c:c + w], preferred_element_type=F32).astype(BF)

    for load in loads[3:]:
        load.wait()
    for k in range(nt):
        pick = picker(meta_t[k, z, pl.ds(t, 1), :])
        for c, w in pieces(width, 512):
            rows[0, k * cap:(k + 1) * cap, c:c + w] = jnp.dot(
                pick, tok_t[k, :, c:c + w], preferred_element_type=F32).astype(BF)

    for k in range(1, nt):
        dispatch_copy(1, k).wait_recv()
    expert(1)
    near_back_copy().start()
    each(1, ne // 2, dispatch_odd)

    def routed_stage(i):
        evens = ne // 2 - 1
        s = jnp.where(i < evens, 2 * i + 2, 2 * (i - evens) + 3)
        s = jnp.where(i == ne - 2, 0, s)

        @pl.when(s > 0)
        def _():
            for k in range(1, nt):
                dispatch_copy(s, k).wait_recv()

        expert(s)

        @pl.when(s > 0)
        def _():
            for k in range(1, nt):
                return_copy(s, k).start()
            back[s, 0:cap] = rows[s, 0:cap]

    each(0, ne - 1, routed_stage)

    flip = (((0,), (0,)), ((), ()))

    def combined(s):
        for k in range(1, nt):
            return_copy(s, k).wait_recv()
        return jnp.concatenate(
            [weigher(meta_z[s, pl.ds(t_peer(k), 1), :], meta_z[s, pl.ds(nt + t_peer(k), 1), :]) for k in range(nt)],
            axis=0,
        )

    def combine_odd(j):
        s = 2 * j + 1
        parts = combined(s)
        for h in range(2):
            for c, w in pieces(width // 2, 512):
                c = c + h * (width // 2)
                tok_z[s, :, c:c + w] = lax.dot_general(
                    parts, back[s, :, c:c + w], flip, preferred_element_type=F32).astype(BF)
            back_near_copy(s, h).start()

    def combine_even(j):
        s = 2 * j
        parts = combined(s)
        forward_copy(s + 1).wait_send()
        for h in range(2):
            back_near_copy(s + 1, h).wait_recv()
            for c, w in pieces(width // 2, 512):
                c = c + h * (width // 2)
                got = lax.dot_general(parts, back[s, :, c:c + w], flip, preferred_element_type=F32)
                tok_z[s, :, c:c + w] = (got + back_z[s + 1, :, c:c + w].astype(F32)).astype(BF)
            back_z_copy(s, h).start()

    for k, h in direct:
        tok_t_copy(k, h).wait_send()
    if relayed:
        for h in range(2):
            relay_copy(h).wait_send()
    near_back_copy().wait_recv()

    for k in ([3, 1, 2, 0] if relayed else [*range(1, nt), 0]):
        own = weigher(meta_t[k, z, pl.ds(t, 1), :], meta_t[k, z, pl.ds(nt + t, 1), :])
        by = z_peer(1)
        other = weigher(meta_t[k, by, pl.ds(t, 1), :], meta_t[k, by, pl.ds(nt + t, 1), :])
        logit = jnp.sum(tok_t[k].astype(F32) * gate_ref[...].astype(F32), axis=1, keepdims=True)
        scale = 1.0 / (1.0 + jnp.exp(-logit))
        span = slice(k * cap, (k + 1) * cap)
        for c, w in pieces(width, 512):
            got = lax.dot_general(own, rows[0, span, c:c + w], flip, preferred_element_type=F32)
            got = got + lax.dot_general(other, back[1, span, c:c + w], flip, preferred_element_type=F32)
            got = got + scale * part_s[k * tok:(k + 1) * tok, c:c + w].astype(F32)
            if k == 0:
                total[:, c:c + w] = got
            elif relayed and k < 3:
                now = slice((1 - k % 2) * half, (2 - k % 2) * half)
                later = slice((k % 2) * half, (k % 2 + 1) * half)
                tok_t[k, now, c:c + w] = got[now].astype(BF)
                held[k - 1, :, c:c + w] = got[later]
            else:
                tok_t[k, :, c:c + w] = got.astype(BF)
        if relayed and k == 3:
            for h in range(2):
                back_relay_copy(h).start()
        elif relayed and k:
            back_t_copy(k, 1 - k % 2).start()
        elif k:
            for h in range(2):
                back_t_copy(k, h).start()
    each(1, ne // 2, combine_odd)
    if relayed:
        for k in (1, 2):
            h = k % 2
            back_relay_copy(h).wait_recv()
            tok_t[k, part_rows(h), :] = (held[k - 1] + back_t[3, part_rows(h), :].astype(F32)).astype(BF)
            back_t_copy(k, h).start()

    each(1, ne // 2, combine_even)

    for k in peers:
        for h in range(2):
            back_t_copy(k, h).wait_recv()
        total[...] += back_t[k].astype(F32)
    for s in range(2, ne, 2):
        for h in range(2):
            back_z_copy(s, h).wait_recv()
        total[...] += back_z[s].astype(F32)
    out_ref[...] = total[...].astype(BF)

    near_back_copy().wait_send()
    for s in range(1, ne):
        meta_z_copy(s).wait_send()
        for k in range(1, nt):
            dispatch_copy(s, k).wait_send()
            if s > 1:
                return_copy(s, k).wait_send()
    for s in own_steps:
        tok_z_copy(s).wait_send()
    for s in range(2, ne, 2):
        for h in range(2):
            back_z_copy(s, h).wait_send()
            back_near_copy(s + 1, h).wait_send()
    for k in range(1, nt):
        meta_t_copy(k).wait_send()
    for k, h in direct:
        back_t_copy(k, h).wait_send()
    if relayed:
        for h in range(2):
            back_relay_copy(h).wait_send()


def per_device(
    tokens, expert_ids, gate_probs, w_gate, w_up, w_down, s_gate, s_up, s_down, shared_gate
):
    tok, width = tokens.shape
    top = expert_ids.shape[1]
    ne = lax.axis_size("expert")
    nt = lax.axis_size("tensor")
    experts = ne * nt
    cap = max(2, 2 * top * tok // experts)
    inner = w_gate.shape[2]
    inner_s = s_gate.shape[1]
    vmem = pl.BlockSpec(memory_space=pltpu.VMEM)
    hbm = pl.BlockSpec(memory_space=pl.ANY)
    dma = pltpu.SemaphoreType.DMA
    group = nt * cap
    return pl.pallas_call(
        functools.partial(layer_kernel, ne, nt, cap),
        out_shape=jax.ShapeDtypeStruct((tok, width), BF),
        in_specs=[hbm, vmem, vmem, hbm, hbm, hbm, hbm, hbm, hbm, vmem],
        out_specs=vmem,
        scratch_shapes=[
            pltpu.VMEM((width, inner), BF),
            pltpu.VMEM((width, inner), BF),
            pltpu.VMEM((inner, width), BF),
            pltpu.VMEM((inner_s, width), BF),
            pltpu.VMEM((inner_s, width), BF),
            pltpu.VMEM((inner_s, width), BF),
            pltpu.VMEM((ne, 2 * nt, tok), F32),
            pltpu.VMEM((ne, 2 * nt, tok), F32),
            pltpu.VMEM((nt, ne, 2 * nt, tok), F32),
            pltpu.VMEM((nt, tok, width), BF),
            pltpu.VMEM((ne, tok, width), BF),
            pltpu.VMEM((ne, group, width), BF),
            pltpu.VMEM((ne, group, width), BF),
            pltpu.VMEM((ne, group, width), BF),
            pltpu.VMEM((nt, tok, width), BF),
            pltpu.VMEM((ne, tok, width), BF),
            pltpu.VMEM((group, inner), BF),
            pltpu.VMEM((nt * tok, inner_s), BF),
            pltpu.VMEM((nt * tok, width), BF),
            pltpu.VMEM((tok, width), F32),
            pltpu.VMEM((2, tok // 2, width), F32),
            dma((7,)),
            dma((ne,)), dma((ne,)), dma((nt,)), dma((nt,)),
            dma((ne,)), dma((ne,)), dma((nt, 2)), dma((nt, 2)),
            dma((ne, nt)), dma((ne, nt)), dma((ne, nt)), dma((ne, nt)),
            dma((nt, 2)), dma((nt, 2)), dma((ne, 2)), dma((ne, 2)),
        ],
        compiler_params=pltpu.CompilerParams(
            collective_id=0, has_side_effects=True, vmem_limit_bytes=67043328
        ),
        name="moe_layer",
    )(
        tokens, expert_ids.T, gate_probs.T, w_gate, w_up, w_down,
        s_gate.T, s_up.T, s_down, shared_gate.reshape(1, width),
    )


def solution(mesh):
    return jax.shard_map(
        per_device,
        mesh=mesh,
        in_specs=(
            P(("dp", "expert", "tensor"), None),
            P(("dp", "expert", "tensor"), None),
            P(("dp", "expert", "tensor"), None),
            P(("expert", "tensor"), None, None),
            P(("expert", "tensor"), None, None),
            P(("expert", "tensor"), None, None),
            P(None, "tensor"),
            P(None, "tensor"),
            P("tensor", None),
            P(),
        ),
        out_specs=P(("dp", "expert", "tensor"), None),
        check_vma=False,
    )
```
